512 devices in a mesh: row: 32 (over z, core), col: 16 (over y, x).
Axes of the slice: x: 4, y: 4, z: 16, core: 2. Of those that a mesh axis runs over, the one named last changes fastest.
Arguments:
- weights: bfloat16 [2, 24576, 6144], P(None, 'row', 'col'), may hold values from -0.15625 to 0.15625
- pattern: int32 [2, 192, 48], P(None, 'row', 'col'), may hold values 0 or 1
- sketch: bfloat16 [6144, 512], P('col'), may hold values from -6 to 6
Outputs:
- basis: float32 [2, 24576, 512], P(None, ('row', 'col'))
The draws below stay inside these ranges and needn't reach their ends.
Inputs may be any that keep to these rules, and one draw needn't show every extreme that they name: `pattern`: 1 marks a block of the sparse part, 0 a block of the residual.
All inputs are finite; a program needn't handle non-finite values.
Results may differ from the reference program's by a relative error of at most 0.0003.
Values sent between devices are 32-bit elements; how exact they have to be, the bound alone decides.
No kernel may reach another device: no remote copies, remote signals or barrier semaphores. Data moves between devices by JAX's collectives and lax.ppermute only.
A program may use at most 64 MiB of HBM per device.

```python
import jax
import jax.numpy as jnp
from jax import lax

M = 24576
N = 6144
K = 512
BLOCK = 128
LAYERS = 2
ROW_BLOCKS = 192
COL_BLOCKS = 48


def set_ends(array, stream_key, least, top_value):
    longest = array.shape.index(max(array.shape))
    spots = []
    for shift in (0, 1):
        where = [jax.random.randint(jax.random.fold_in(stream_key, axis), (), 0, length) for axis, length in enumerate(array.shape)]
        where[longest] = (where[longest] + shift) % array.shape[longest]
        spots.append(tuple(where))
    return array.at[spots[0]].set(least).at[spots[1]].set(top_value)


def with_spikes(entries, rng, source, target, shards_of, factor):
    def block_of(dim):
        return (jnp.arange(entries.shape[dim]) // (entries.shape[dim] // shards_of)).reshape((-1,) + (1,) * (entries.ndim - 1 - dim))

    first = jax.random.permutation(rng, shards_of)[block_of(target)]
    far = (block_of(target) + shards_of // 2) % shards_of
    return jnp.where((block_of(source) == first) | (block_of(source) == far), factor * entries, entries)


def block_levels(stream_key, dims, cuts, least, largest):
    def one(position, shards_of):
        heights = jax.random.uniform(jax.random.fold_in(jax.random.fold_in(stream_key, 6), position), (shards_of,), jnp.float32, least / len(cuts), largest / len(cuts))
        return jnp.repeat(jnp.exp(heights), dims[position] // shards_of).reshape((-1,) + (1,) * (len(dims) - position - 1))

    factor_of = one(*cuts[0])
    for cut in cuts[1:]:
        factor_of = factor_of * one(*cut)
    return factor_of


def normal_values(own_key, shape, width, limit, cuts=(), kind=jnp.bfloat16):
    drawn = width * jax.random.normal(own_key, shape, jnp.float32)
    if cuts:
        drawn = drawn * block_levels(own_key, shape, cuts, -0.22, 0.18)
    return jnp.clip(drawn, -limit, limit).astype(kind)


def gaussian_with(key, extent, spread, most, split, heavy, kind=jnp.bfloat16):
    result = spread * jax.random.normal(key, extent, jnp.float32)
    if split:
        result = result * block_levels(key, extent, split, -0.22, 0.18)
    return jnp.clip(with_spikes(result, jax.random.fold_in(key, 3), *heavy), -most, most).astype(kind)


def setup_inputs(seed: int = 0) -> dict:
    splits = jax.random.split(jax.random.key(seed), 4)
    return {
        "weights": gaussian_with(splits[0], (LAYERS, M, N), N ** -0.5, 0.15625, ((1, 32), (2, 16)), (2, 1, 32, 2.75)),
        "pattern": set_ends((jax.random.randint(splits[1], (LAYERS, ROW_BLOCKS, COL_BLOCKS), 0, 2) < 1).astype(jnp.int32), jax.random.fold_in(splits[1], 1), 0, 1),
        "sketch": normal_values(splits[2], (N, K), 1.0, 6.0, ((0, 16),)),
    }


def one_layer(weight, marks, sketch):
    keep = (1 - marks).astype(weight.dtype)
    shaped = weight.reshape(ROW_BLOCKS, BLOCK, COL_BLOCKS, BLOCK) * keep[:, None, :, None]
    leftover = shaped.reshape(M, N)
    sampled = jnp.dot(leftover.astype(jnp.float32), sketch.astype(jnp.float32), preferred_element_type=jnp.float32)
    gram = lax.dot_general(sampled.astype(jnp.float32), sampled.astype(jnp.float32), (((0,), (0,)), ((), ())), precision=lax.Precision.HIGHEST, preferred_element_type=jnp.float32) / M
    lower = jnp.linalg.cholesky(gram)
    solved = lax.linalg.triangular_solve(lower, sampled, left_side=False, lower=True, transpose_a=True)
    return solved * jnp.sqrt(jnp.float32(M))

def reference(weights, pattern, sketch):
    outputs = [one_layer(weights[layer], pattern[layer], sketch) for layer in range(LAYERS)]
    return jnp.stack(outputs, axis=0)
```

```python
import jax
import jax.numpy as jnp
from jax import lax
from jax.experimental import pallas as pl
from jax.experimental.pallas import tpu as pltpu
from jax.sharding import PartitionSpec as P

M = 24576
BLOCK = 128
LAYERS = 2
SUP = 32
PAN = 8
HI = lax.Precision.HIGHEST


def nt(a, b):
    return lax.dot_general(a, b, (((1,), (1,)), ((), ())), precision=HI, preferred_element_type=jnp.float32)
def tn(a, b):
    return lax.dot_general(a, b, (((0,), (0,)), ((), ())), precision=HI, preferred_element_type=jnp.float32)

def inverse_factor(x_ref):
    lane8 = lax.broadcasted_iota(jnp.int32, (PAN, BLOCK), 1)
    row8 = lax.broadcasted_iota(jnp.int32, (PAN, BLOCK), 0)
    for first in range(0, BLOCK, SUP):
        rows = [x_ref[first + PAN * i : first + PAN * (i + 1), :] for i in range(SUP // PAN)]
        for p in range(SUP // PAN):
            lead = first + PAN * p
            cols = [[jnp.broadcast_to(rows[i][:, lead + k : lead + k + 1], (PAN, BLOCK)) for k in range(PAN)] for i in range(p, SUP // PAN)]
            diag = jnp.ones((PAN, BLOCK), jnp.float32)
            for k in range(PAN):
                pivot = jnp.broadcast_to(cols[0][k][k : k + 1, :], (PAN, BLOCK))
                inv = 1.0 / pivot
                diag = jnp.where(row8 == k, pivot, diag)
                source = jnp.where(lane8 == lead + k, 1.0, jnp.broadcast_to(rows[p][k : k + 1, :], (PAN, BLOCK)))
                heads = [jnp.broadcast_to(cols[0][m][k : k + 1, :], (PAN, BLOCK)) * inv for m in range(k + 1, PAN)]
                for i in range(p, SUP // PAN):
                    col = cols[i - p][k]
                    if i == p:
                        col = jnp.where(row8 > k, col, 0.0)
                        keep = jnp.where((lane8 == lead + k) & (row8 > k), 0.0, rows[i])
                        keep = jnp.where((lane8 == lead + k) & (row8 == k), 1.0, keep)
                    else:
                        keep = jnp.where(lane8 == lead + k, 0.0, rows[i])
                    rows[i] = keep - (col * inv) * source
                    for m in range(k + 1, PAN):
                        cols[i - p][m] = cols[i - p][m] - col * heads[m - k - 1]
            rows[p] = rows[p] * lax.rsqrt(diag)
        whole = jnp.concatenate(rows, axis=0)
        lane = lax.broadcasted_iota(jnp.int32, (SUP, BLOCK), 1)
        row = lax.broadcasted_iota(jnp.int32, (SUP, BLOCK), 0) + first
        low = jnp.where((lane > row) & (lane < first + SUP), 0.0, whole)
        last = first + SUP
        if last < BLOCK:
            x_ref[first:last, :] = jnp.where(lane > row, 0.0, whole)
            delta = tn(whole, low)
            lane_b = lax.broadcasted_iota(jnp.int32, (BLOCK - last, BLOCK), 1)
            below = x_ref[last:BLOCK, :]
            below = jnp.where((lane_b >= first) & (lane_b < last), 0.0, below)
            x_ref[last:BLOCK, :] = below - delta[last:BLOCK, :]
        else:
            x_ref[first:last, :] = low
    return x_ref[...]

def start_of(n, j):
    return BLOCK * sum(n - i for i in range(j))

def basis_kernel(gram_ref, rows_ref, out_ref, a_ref, s_ref, x_ref):
    n = rows_ref.shape[1] // BLOCK
    a_ref[...] = gram_ref[...]
    s_ref[...] = rows_ref[...]
    for k in range(n):
        base = start_of(n, k)
        x_ref[...] = a_ref[base : base + BLOCK, :]
        w = inverse_factor(x_ref)
        tail = s_ref[:, k * BLOCK : (k + 1) * BLOCK]
        below = (n - 1 - k) * BLOCK
        if below:
            stacked = jnp.concatenate([a_ref[base + BLOCK : base + BLOCK + below, :], tail], axis=0)
        else:
            stacked = tail
        panel = nt(stacked, w)
        out_ref[:, k * BLOCK : (k + 1) * BLOCK] = panel[below:, :] * float(M)
        for j in range(k + 1, n):
            off = (j - k - 1) * BLOCK
            update = nt(panel[off:, :], panel[off : off + BLOCK, :])
            height = (n - j) * BLOCK
            to = start_of(n, j)
            a_ref[to : to + height, :] = a_ref[to : to + height, :] - update[:height, :]
            s_ref[:, j * BLOCK : (j + 1) * BLOCK] = s_ref[:, j * BLOCK : (j + 1) * BLOCK] - update[height:, :]

def basis(gram, rows):
    return pl.pallas_call(
        basis_kernel,
        out_shape=jax.ShapeDtypeStruct(rows.shape, jnp.float32),
        in_specs=[vmem(), vmem()],
        out_specs=vmem(),
        scratch_shapes=[pltpu.VMEM(gram.shape, jnp.float32), pltpu.VMEM(rows.shape, jnp.float32), pltpu.VMEM((BLOCK, BLOCK), jnp.float32)],
        name="basis",
    )(gram, rows)


def vmem():
    return pl.BlockSpec(memory_space=pltpu.VMEM)


def product_kernel(pattern_ref, weights_ref, sketch_ref, out_ref):
    layer = pl.program_id(0)
    height, width = weights_ref.shape[1:]
    strips = []
    for i in range(height // BLOCK):
        parts = []
        for j in range(width // BLOCK):
            block = weights_ref[0, i * BLOCK : (i + 1) * BLOCK, j * BLOCK : (j + 1) * BLOCK]
            parts.append(jnp.where(pattern_ref[layer, i, j] == 1, jnp.zeros_like(block), block))
        strips.append(jnp.concatenate(parts, axis=1))
    leftover = jnp.concatenate(strips, axis=0)
    product = jnp.dot(leftover, sketch_ref[...], preferred_element_type=jnp.float32)
    out_ref[...] = product.reshape(out_ref.shape)


def product(weights, pattern, sketch, peers):
    layers, height, width = weights.shape
    rank = sketch.shape[1]
    share = height // peers
    return pl.pallas_call(
        product_kernel,
        grid=(layers,),
        out_shape=jax.ShapeDtypeStruct((peers, layers, share, rank), jnp.float32),
        in_specs=[
            pl.BlockSpec(memory_space=pltpu.SMEM),
            pl.BlockSpec((1, height, width), lambda l: (l, 0, 0)),
            pl.BlockSpec((width, rank), lambda l: (0, 0)),
        ],
        out_specs=pl.BlockSpec((peers, 1, share, rank), lambda l: (0, l, 0, 0)),
        name="product",
    )(pattern, weights, sketch)


def gram_kernel(mine_ref, got_ref, gram_ref, rows_ref):
    rows = jnp.concatenate([mine_ref[...], got_ref[...]], axis=0)
    rows_ref[...] = rows
    n = rows.shape[1] // BLOCK
    for j in range(n):
        to = start_of(n, j)
        gram_ref[to : to + (n - j) * BLOCK, :] = tn(rows[:, j * BLOCK :], rows[:, j * BLOCK : (j + 1) * BLOCK])


def local_gram(mine, got):
    share, rank = mine.shape
    n = rank // BLOCK
    return pl.pallas_call(
        gram_kernel,
        out_shape=(
            jax.ShapeDtypeStruct((start_of(n, n), BLOCK), jnp.float32),
            jax.ShapeDtypeStruct((2 * share, rank), jnp.float32),
        ),
        in_specs=[vmem(), vmem()],
        out_specs=(vmem(), vmem()),
        name="local_gram",
    )(mine, got)


def make_body(row_size, peers):
    chips = row_size // 2
    cores = [(2 * z + c, 2 * z + 1 - c) for z in range(chips) for c in range(2)]
    groups = [[2 * z + c for z in range(chips)] for c in range(2)]

    def to_col(x):
        return lax.all_to_all(x, "col", 0, 0)

    def to_chips(x):
        return lax.all_to_all(x, "row", 0, 0, axis_index_groups=groups)

    def summed_gram(gram):
        height = gram.shape[0] // peers
        piece = jnp.sum(to_col(gram.reshape(peers, height, BLOCK)), axis=0)
        part = jnp.sum(to_chips(piece.reshape(chips, height // chips, BLOCK)), axis=0)
        piece = to_chips(jnp.broadcast_to(part, (chips, *part.shape))).reshape(height, BLOCK)
        return to_col(jnp.broadcast_to(piece, (peers, *piece.shape))).reshape(gram.shape)

    def body(weights, pattern, sketch):
        second = (lax.axis_index("row") % 2) == 1
        partial = product(weights, pattern, sketch, peers)
        sampled = jnp.sum(to_col(partial), axis=0)
        mine = jnp.where(second, sampled[1], sampled[0])
        other = jnp.where(second, sampled[0], sampled[1])
        got = lax.ppermute(other, "row", cores)
        gram, rows = local_gram(mine, got)
        out = basis(summed_gram(gram), rows)
        share = mine.shape[0]
        own, away = out[:share], out[share:]
        back = lax.ppermute(away, "row", cores)
        return jnp.stack([jnp.where(second, back, own), jnp.where(second, own, back)], axis=0)

    return body


def solution(mesh):
    return jax.shard_map(
        make_body(mesh.shape["row"], mesh.shape["col"]),
        mesh=mesh,
        in_specs=(P(None, "row", "col"), P(None, "row", "col"), P("col", None)),
        out_specs=P(None, ("row", "col"), None),
        check_vma=False,
    )
```

```python
import jax
import jax.numpy as jnp
from jax import lax
from jax.experimental import pallas as pl
from jax.experimental.pallas import tpu as pltpu
from jax.sharding import PartitionSpec as P

M = 24576
BLOCK = 128
LAYERS = 2
SUP = 32
PAN = 8
GRANT = 24 << 20
HI = lax.Precision.HIGHEST


def nt(a, b):
    return lax.dot_general(a, b, (((1,), (1,)), ((), ())), precision=HI, preferred_element_type=jnp.float32)
def tn(a, b):
    return lax.dot_general(a, b, (((0,), (0,)), ((), ())), precision=HI, preferred_element_type=jnp.float32)

def inverse_factor(x_ref):
    lane8 = lax.broadcasted_iota(jnp.int32, (PAN, BLOCK), 1)
    row8 = lax.broadcasted_iota(jnp.int32, (PAN, BLOCK), 0)
    for first in range(0, BLOCK, SUP):
        rows = [x_ref[first + PAN * i : first + PAN * (i + 1), :] for i in range(SUP // PAN)]
        for p in range(SUP // PAN):
            lead = first + PAN * p
            cols = [[jnp.broadcast_to(rows[i][:, lead + k : lead + k + 1], (PAN, BLOCK)) for k in range(PAN)] for i in range(p, SUP // PAN)]
            diag = jnp.ones((PAN, BLOCK), jnp.float32)
            for k in range(PAN):
                pivot = jnp.broadcast_to(cols[0][k][k : k + 1, :], (PAN, BLOCK))
                inv = 1.0 / pivot
                diag = jnp.where(row8 == k, pivot, diag)
                source = jnp.where(lane8 == lead + k, 1.0, jnp.broadcast_to(rows[p][k : k + 1, :], (PAN, BLOCK)))
                heads = [jnp.broadcast_to(cols[0][m][k : k + 1, :], (PAN, BLOCK)) * inv for m in range(k + 1, PAN)]
                for i in range(p, SUP // PAN):
                    col = cols[i - p][k]
                    if i == p:
                        col = jnp.where(row8 > k, col, 0.0)
                        keep = jnp.where((lane8 == lead + k) & (row8 > k), 0.0, rows[i])
                        keep = jnp.where((lane8 == lead + k) & (row8 == k), 1.0, keep)
                    else:
                        keep = jnp.where(lane8 == lead + k, 0.0, rows[i])
                    rows[i] = keep - (col * inv) * source
                    for m in range(k + 1, PAN):
                        cols[i - p][m] = cols[i - p][m] - col * heads[m - k - 1]
            rows[p] = rows[p] * lax.rsqrt(diag)
        whole = jnp.concatenate(rows, axis=0)
        lane = lax.broadcasted_iota(jnp.int32, (SUP, BLOCK), 1)
        row = lax.broadcasted_iota(jnp.int32, (SUP, BLOCK), 0) + first
        low = jnp.where((lane > row) & (lane < first + SUP), 0.0, whole)
        last = first + SUP
        if last < BLOCK:
            x_ref[first:last, :] = jnp.where(lane > row, 0.0, whole)
            delta = tn(whole, low)
            lane_b = lax.broadcasted_iota(jnp.int32, (BLOCK - last, BLOCK), 1)
            below = x_ref[last:BLOCK, :]
            below = jnp.where((lane_b >= first) & (lane_b < last), 0.0, below)
            x_ref[last:BLOCK, :] = below - delta[last:BLOCK, :]
        else:
            x_ref[first:last, :] = low
    return x_ref[...]

def start_of(n, j):
    return BLOCK * sum(n - i for i in range(j))

def basis_kernel(gram_ref, rows_ref, own_ref, away_ref, a_ref, s_ref, x_ref):
    n = rows_ref.shape[1] // BLOCK
    a_ref[...] = gram_ref[...]
    s_ref[...] = rows_ref[...]
    for k in range(n):
        base = start_of(n, k)
        x_ref[...] = a_ref[base : base + BLOCK, :]
        w = inverse_factor(x_ref)
        tail = s_ref[:, k * BLOCK : (k + 1) * BLOCK]
        below = (n - 1 - k) * BLOCK
        if below:
            stacked = jnp.concatenate([a_ref[base + BLOCK : base + BLOCK + below, :], tail], axis=0)
        else:
            stacked = tail
        panel = nt(stacked, w)
        solved = panel[below:, :] * float(M)
        share = solved.shape[0] // 2
        own_ref[:, k * BLOCK : (k + 1) * BLOCK] = solved[:share, :]
        away_ref[:, k * BLOCK : (k + 1) * BLOCK] = solved[share:, :]
        for j in range(k + 1, n):
            off = (j - k - 1) * BLOCK
            update = nt(panel[off:, :], panel[off : off + BLOCK, :])
            height = (n - j) * BLOCK
            to = start_of(n, j)
            a_ref[to : to + height, :] = a_ref[to : to + height, :] - update[:height, :]
            s_ref[:, j * BLOCK : (j + 1) * BLOCK] = s_ref[:, j * BLOCK : (j + 1) * BLOCK] - update[height:, :]

def basis(gram, rows):
    return pl.pallas_call(
        basis_kernel,
        out_shape=(in_vmem((rows.shape[0] // 2, rows.shape[1])),) * 2,
        in_specs=[vmem(), vmem()],
        out_specs=(vmem(), vmem()),
        compiler_params=pltpu.CompilerParams(vmem_limit_bytes=GRANT),
        scratch_shapes=[pltpu.VMEM(gram.shape, jnp.float32), pltpu.VMEM(rows.shape, jnp.float32), pltpu.VMEM((BLOCK, BLOCK), jnp.float32)],
        name="basis",
    )(gram, rows)


def vmem():
    return pl.BlockSpec(memory_space=pltpu.VMEM)


def in_vmem(shape):
    return pltpu.VMEM(shape, jnp.float32)


def held(x):
    return pltpu.with_memory_space_constraint(x, pltpu.VMEM)


def product_kernel(pattern_ref, weights_ref, sketch_ref, out_ref):
    layers, height, width = weights_ref.shape
    peers, _, share, rank = out_ref.shape
    for layer in range(layers):
        strips = []
        for i in range(height // BLOCK):
            parts = []
            for j in range(width // BLOCK):
                block = weights_ref[layer, i * BLOCK : (i + 1) * BLOCK, j * BLOCK : (j + 1) * BLOCK]
                parts.append(jnp.where(pattern_ref[j, layer, i] == 1, jnp.zeros_like(block), block))
            strips.append(jnp.concatenate(parts, axis=1))
        leftover = jnp.concatenate(strips, axis=0)
        product = jnp.dot(leftover, sketch_ref[...], preferred_element_type=jnp.float32)
        out_ref[:, layer] = product.reshape(peers, share, rank)


def product(weights, pattern, sketch, peers):
    layers, height, width = weights.shape
    rank = sketch.shape[1]
    return pl.pallas_call(
        product_kernel,
        out_shape=in_vmem((peers, layers, height // peers, rank)),
        in_specs=[pl.BlockSpec(memory_space=pltpu.SMEM), vmem(), vmem()],
        out_specs=vmem(),
        compiler_params=pltpu.CompilerParams(vmem_limit_bytes=GRANT),
        name="product",
    )(pattern, weights, sketch)


def total_kernel(core_ref, parts_ref, mine_ref, other_ref):
    core = core_ref[0]
    peers = parts_ref.shape[0]
    for layer, out_ref in ((core, mine_ref), (1 - core, other_ref)):
        total = parts_ref[0, layer]
        for peer in range(1, peers):
            total = total + parts_ref[peer, layer]
        out_ref[...] = total


def total(core, parts):
    shape = in_vmem(parts.shape[2:])
    return pl.pallas_call(
        total_kernel,
        out_shape=(shape, shape),
        in_specs=[pl.BlockSpec(memory_space=pltpu.SMEM), vmem()],
        out_specs=(vmem(), vmem()),
        compiler_params=pltpu.CompilerParams(vmem_limit_bytes=GRANT),
        name="total",
    )(core, held(parts))


def merge_kernel(core_ref, own_ref, back_ref, out_ref):
    core = core_ref[0]
    out_ref[core] = own_ref[...]
    out_ref[1 - core] = back_ref[...]


def merge(core, own, back):
    return pl.pallas_call(
        merge_kernel,
        out_shape=jax.ShapeDtypeStruct((LAYERS, *own.shape), jnp.float32),
        in_specs=[pl.BlockSpec(memory_space=pltpu.SMEM), vmem(), vmem()],
        out_specs=vmem(),
        compiler_params=pltpu.CompilerParams(vmem_limit_bytes=GRANT),
        name="merge",
    )(core, held(own), held(back))


def gram_kernel(mine_ref, got_ref, gram_ref, rows_ref):
    rows = jnp.concatenate([mine_ref[...], got_ref[...]], axis=0)
    rows_ref[...] = rows
    n = rows.shape[1] // BLOCK
    for j in range(n):
        to = start_of(n, j)
        gram_ref[to : to + (n - j) * BLOCK, :] = tn(rows[:, j * BLOCK :], rows[:, j * BLOCK : (j + 1) * BLOCK])


def local_gram(mine, got):
    share, rank = mine.shape
    n = rank // BLOCK
    return pl.pallas_call(
        gram_kernel,
        out_shape=(
            in_vmem((start_of(n, n), BLOCK)),
            in_vmem((2 * share, rank)),
        ),
        in_specs=[vmem(), vmem()],
        out_specs=(vmem(), vmem()),
        compiler_params=pltpu.CompilerParams(vmem_limit_bytes=GRANT),
        name="local_gram",
    )(held(mine), held(got))


def make_body(row_size, peers):
    chips = row_size // 2
    cores = [(2 * z + c, 2 * z + 1 - c) for z in range(chips) for c in range(2)]
    groups = [[2 * z + c for z in range(chips)] for c in range(2)]

    def to_col(x):
        return lax.all_to_all(x, "col", 0, 0)

    def to_chips(x):
        return lax.all_to_all(x, "row", 0, 0, axis_index_groups=groups)

    def summed_gram(gram):
        height = gram.shape[0] // peers
        piece = jnp.sum(to_col(gram.reshape(peers, height, BLOCK)), axis=0)
        part = jnp.sum(to_chips(piece.reshape(chips, height // chips, BLOCK)), axis=0)
        piece = to_chips(jnp.broadcast_to(part, (chips, *part.shape))).reshape(height, BLOCK)
        return to_col(jnp.broadcast_to(piece, (peers, *piece.shape))).reshape(gram.shape)

    def body(weights, pattern, sketch):
        core = (lax.axis_index("row") % 2).astype(jnp.int32).reshape(1)
        pattern, core = lax.optimization_barrier((pattern.transpose(2, 0, 1), core))
        mine, other = total(core, to_col(product(weights, pattern, sketch, peers)))
        got = lax.ppermute(other, "row", cores)
        gram, rows = local_gram(mine, got)
        own, away = basis(held(summed_gram(gram)), held(rows))
        back = lax.ppermute(away, "row", cores)
        return merge(core, own, back)

    return body


def solution(mesh):
    return jax.shard_map(
        make_body(mesh.shape["row"], mesh.shape["col"]),
        mesh=mesh,
        in_specs=(P(None, "row", "col"), P(None, "row", "col"), P("col", None)),
        out_specs=P(None, ("row", "col"), None),
        check_vma=False,
    )
```

```python
import math

import jax
import jax.numpy as jnp
from jax import lax
from jax.experimental import pallas as pl
from jax.experimental.pallas import tpu as pltpu
from jax.sharding import PartitionSpec as P

M = 24576
BLOCK = 128
LAYERS = 2
SUP = 32
PAN = 8
GRANT = 24 << 20
HI = lax.Precision.HIGHEST


def nt(a, b):
    return lax.dot_general(a, b, (((1,), (1,)), ((), ())), precision=HI, preferred_element_type=jnp.float32)
def tn(a, b):
    return lax.dot_general(a, b, (((0,), (0,)), ((), ())), precision=HI, preferred_element_type=jnp.float32)

def inverse_factor(x_ref):
    lane8 = lax.broadcasted_iota(jnp.int32, (PAN, BLOCK), 1)
    row8 = lax.broadcasted_iota(jnp.int32, (PAN, BLOCK), 0)
    for first in range(0, BLOCK, SUP):
        rows = [x_ref[first + PAN * i : first + PAN * (i + 1), :] for i in range(SUP // PAN)]
        for p in range(SUP // PAN):
            lead = first + PAN * p
            cols = [[jnp.broadcast_to(rows[i][:, lead + k : lead + k + 1], (PAN, BLOCK)) for k in range(PAN)] for i in range(p, SUP // PAN)]
            diag = jnp.ones((PAN, BLOCK), jnp.float32)
            for k in range(PAN):
                pivot = jnp.broadcast_to(cols[0][k][k : k + 1, :], (PAN, BLOCK))
                inv = 1.0 / pivot
                diag = jnp.where(row8 == k, pivot, diag)
                source = jnp.where(lane8 == lead + k, 1.0, jnp.broadcast_to(rows[p][k : k + 1, :], (PAN, BLOCK)))
                heads = [jnp.broadcast_to(cols[0][m][k : k + 1, :], (PAN, BLOCK)) * inv for m in range(k + 1, PAN)]
                for i in range(p, SUP // PAN):
                    col = cols[i - p][k]
                    if i == p:
                        col = jnp.where(row8 > k, col, 0.0)
                        keep = jnp.where((lane8 == lead + k) & (row8 > k), 0.0, rows[i])
                        keep = jnp.where((lane8 == lead + k) & (row8 == k), 1.0, keep)
                    else:
                        keep = jnp.where(lane8 == lead + k, 0.0, rows[i])
                    rows[i] = keep - (col * inv) * source
                    for m in range(k + 1, PAN):
                        cols[i - p][m] = cols[i - p][m] - col * heads[m - k - 1]
            rows[p] = rows[p] * lax.rsqrt(diag)
        whole = jnp.concatenate(rows, axis=0)
        lane = lax.broadcasted_iota(jnp.int32, (SUP, BLOCK), 1)
        row = lax.broadcasted_iota(jnp.int32, (SUP, BLOCK), 0) + first
        low = jnp.where((lane > row) & (lane < first + SUP), 0.0, whole)
        last = first + SUP
        if last < BLOCK:
            x_ref[first:last, :] = jnp.where(lane > row, 0.0, whole)
            delta = tn(whole, low)
            lane_b = lax.broadcasted_iota(jnp.int32, (BLOCK - last, BLOCK), 1)
            below = x_ref[last:BLOCK, :]
            below = jnp.where((lane_b >= first) & (lane_b < last), 0.0, below)
            x_ref[last:BLOCK, :] = below - delta[last:BLOCK, :]
        else:
            x_ref[first:last, :] = low
    return x_ref[...]

def start_of(n, j):
    return BLOCK * sum(n - i for i in range(j))

def basis_kernel(gram_ref, rows_ref, own_ref, away_ref, a_ref, s_ref, x_ref):
    n = rows_ref.shape[1] // BLOCK
    a_ref[...] = gram_ref[...]
    s_ref[...] = rows_ref[...]
    for k in range(n):
        base = start_of(n, k)
        x_ref[...] = a_ref[base : base + BLOCK, :]
        w = inverse_factor(x_ref)
        tail = s_ref[:, k * BLOCK : (k + 1) * BLOCK]
        below = (n - 1 - k) * BLOCK
        if below:
            stacked = jnp.concatenate([a_ref[base + BLOCK : base + BLOCK + below, :], tail], axis=0)
        else:
            stacked = tail
        panel = nt(stacked, w)
        solved = panel[below:, :] * float(M)
        share = solved.shape[0] // 2
        own_ref[:, k * BLOCK : (k + 1) * BLOCK] = solved[:share, :]
        away_ref[:, k * BLOCK : (k + 1) * BLOCK] = solved[share:, :]
        for j in range(k + 1, n):
            off = (j - k - 1) * BLOCK
            update = nt(panel[off:, :], panel[off : off + BLOCK, :])
            height = (n - j) * BLOCK
            to = start_of(n, j)
            a_ref[to : to + height, :] = a_ref[to : to + height, :] - update[:height, :]
            s_ref[:, j * BLOCK : (j + 1) * BLOCK] = s_ref[:, j * BLOCK : (j + 1) * BLOCK] - update[height:, :]

def basis(gram, rows):
    return pl.pallas_call(
        basis_kernel,
        out_shape=(in_vmem((rows.shape[0] // 2, rows.shape[1])),) * 2,
        in_specs=[vmem(), vmem()],
        out_specs=(vmem(), vmem()),
        compiler_params=pltpu.CompilerParams(vmem_limit_bytes=GRANT),
        scratch_shapes=[pltpu.VMEM(gram.shape, jnp.float32), pltpu.VMEM(rows.shape, jnp.float32), pltpu.VMEM((BLOCK, BLOCK), jnp.float32)],
        name="basis",
    )(gram, rows)


def vmem():
    return pl.BlockSpec(memory_space=pltpu.VMEM)


def in_vmem(shape):
    return pltpu.VMEM(shape, jnp.float32)


def held(x):
    return pltpu.with_memory_space_constraint(x, pltpu.VMEM)


def product_kernel(pattern_ref, weights_ref, sketch_ref, out_ref):
    layers, height, width = weights_ref.shape
    peers, _, share, rank = out_ref.shape
    for layer in range(layers):
        strips = []
        for i in range(height // BLOCK):
            parts = []
            for j in range(width // BLOCK):
                block = weights_ref[layer, i * BLOCK : (i + 1) * BLOCK, j * BLOCK : (j + 1) * BLOCK]
                parts.append(jnp.where(pattern_ref[j, layer, i] == 1, jnp.zeros_like(block), block))
            strips.append(jnp.concatenate(parts, axis=1))
        leftover = jnp.concatenate(strips, axis=0)
        product = jnp.dot(leftover, sketch_ref[...], preferred_element_type=jnp.float32)
        out_ref[:, layer] = product.reshape(peers, share, rank)


def product(weights, pattern, sketch, peers):
    layers, height, width = weights.shape
    rank = sketch.shape[1]
    return pl.pallas_call(
        product_kernel,
        out_shape=in_vmem((peers, layers, height // peers, rank)),
        in_specs=[pl.BlockSpec(memory_space=pltpu.SMEM), vmem(), vmem()],
        out_specs=vmem(),
        compiler_params=pltpu.CompilerParams(vmem_limit_bytes=GRANT),
        name="product",
    )(pattern, weights, sketch)


def total_kernel(core_ref, parts_ref, mine_ref, other_ref):
    core = core_ref[0]
    peers = parts_ref.shape[0]
    for layer, out_ref in ((core, mine_ref), (1 - core, other_ref)):
        total = parts_ref[0, layer]
        for peer in range(1, peers):
            total = total + parts_ref[peer, layer]
        out_ref[...] = total


def total(core, parts):
    shape = in_vmem(parts.shape[2:])
    return pl.pallas_call(
        total_kernel,
        out_shape=(shape, shape),
        in_specs=[pl.BlockSpec(memory_space=pltpu.SMEM), vmem()],
        out_specs=(vmem(), vmem()),
        compiler_params=pltpu.CompilerParams(vmem_limit_bytes=GRANT),
        name="total",
    )(core, held(parts))


def merge_kernel(core_ref, own_ref, back_ref, out_ref):
    core = core_ref[0]
    out_ref[core] = own_ref[...]
    out_ref[1 - core] = back_ref[...]


def merge(core, own, back):
    return pl.pallas_call(
        merge_kernel,
        out_shape=jax.ShapeDtypeStruct((LAYERS, *own.shape), jnp.float32),
        in_specs=[pl.BlockSpec(memory_space=pltpu.SMEM), vmem(), vmem()],
        out_specs=vmem(),
        compiler_params=pltpu.CompilerParams(vmem_limit_bytes=GRANT),
        name="merge",
    )(core, held(own), held(back))


def gram_kernel(mine_ref, got_ref, gram_ref, rows_ref):
    rows = jnp.concatenate([mine_ref[...], got_ref[...]], axis=0)
    rows_ref[...] = rows
    n = rows.shape[1] // BLOCK
    for j in range(n):
        to = start_of(n, j)
        gram_ref[to : to + (n - j) * BLOCK, :] = tn(rows[:, j * BLOCK :], rows[:, j * BLOCK : (j + 1) * BLOCK])


def local_gram(mine, got):
    share, rank = mine.shape
    n = rank // BLOCK
    return pl.pallas_call(
        gram_kernel,
        out_shape=(
            in_vmem((start_of(n, n), BLOCK)),
            in_vmem((2 * share, rank)),
        ),
        in_specs=[vmem(), vmem()],
        out_specs=(vmem(), vmem()),
        compiler_params=pltpu.CompilerParams(vmem_limit_bytes=GRANT),
        name="local_gram",
    )(held(mine), held(got))


def make_body(row_size, peers):
    chips = row_size // 2
    cores = [(2 * z + c, 2 * z + 1 - c) for z in range(chips) for c in range(2)]
    near = math.isqrt(chips)
    far = chips // near
    near_groups = [[2 * (h * near + l) + c for l in range(near)] for h in range(far) for c in range(2)]
    far_groups = [[2 * (h * near + l) + c for h in range(far)] for l in range(near) for c in range(2)]

    def to_col(x):
        return lax.all_to_all(x, "col", 0, 0)

    def to_near(x):
        return lax.all_to_all(x, "row", 0, 0, axis_index_groups=near_groups)

    def to_far(x):
        return lax.all_to_all(x, "row", 0, 0, axis_index_groups=far_groups)

    def spread(x, exchange, count):
        return exchange(jnp.broadcast_to(x, (count, *x.shape)))

    def summed_gram(gram):
        piece = jnp.sum(to_col(gram.reshape(peers, gram.shape[0] // peers, BLOCK)), axis=0)
        piece = jnp.sum(spread(piece, to_near, near), axis=0)
        piece = jnp.sum(spread(piece, to_far, far), axis=0)
        return spread(piece, to_col, peers).reshape(gram.shape)

    def body(weights, pattern, sketch):
        core = (lax.axis_index("row") % 2).astype(jnp.int32).reshape(1)
        pattern, core = lax.optimization_barrier((pattern.transpose(2, 0, 1), core))
        mine, other = total(core, to_col(product(weights, pattern, sketch, peers)))
        got = lax.ppermute(other, "row", cores)
        gram, rows = local_gram(mine, got)
        own, away = basis(held(summed_gram(gram)), held(rows))
        back = lax.ppermute(away, "row", cores)
        return merge(core, own, back)

    return body


def solution(mesh):
    return jax.shard_map(
        make_body(mesh.shape["row"], mesh.shape["col"]),
        mesh=mesh,
        in_specs=(P(None, "row", "col"), P(None, "row", "col"), P("col", None)),
        out_specs=P(None, ("row", "col"), None),
        check_vma=False,
    )
```

```python
import math

import jax
import jax.numpy as jnp
from jax import lax
from jax.experimental import pallas as pl
from jax.experimental.pallas import tpu as pltpu
from jax.sharding import PartitionSpec as P

M = 24576
BLOCK = 128
LAYERS = 2
SUP = 32
PAN = 16
GRANT = 24 << 20
HI = lax.Precision.HIGHEST


def nt(a, b):
    return lax.dot_general(a, b, (((1,), (1,)), ((), ())), precision=HI, preferred_element_type=jnp.float32)
def tn(a, b):
    return lax.dot_general(a, b, (((0,), (0,)), ((), ())), precision=HI, preferred_element_type=jnp.float32)

def inverse_factor(x_ref):
    lanes = lax.broadcasted_iota(jnp.int32, (PAN, BLOCK), 1)
    rowis = lax.broadcasted_iota(jnp.int32, (PAN, BLOCK), 0)
    for first in range(0, BLOCK, SUP):
        rows = [x_ref[first + PAN * i : first + PAN * (i + 1), :] for i in range(SUP // PAN)]
        for p in range(SUP // PAN):
            lead = first + PAN * p
            cols = [[jnp.broadcast_to(rows[i][:, lead + k : lead + k + 1], (PAN, BLOCK)) for k in range(PAN)] for i in range(p, SUP // PAN)]
            diag = jnp.ones((PAN, BLOCK), jnp.float32)
            for k in range(PAN):
                pivot = jnp.broadcast_to(cols[0][k][k : k + 1, :], (PAN, BLOCK))
                inv = 1.0 / pivot
                diag = jnp.where(rowis == k, pivot, diag)
                source = jnp.where(lanes == lead + k, 1.0, jnp.broadcast_to(rows[p][k : k + 1, :], (PAN, BLOCK)))
                raw = [jnp.broadcast_to(cols[0][k][m : m + 1, :], (PAN, BLOCK)) for m in range(k + 1, PAN)]
                for i in range(p, SUP // PAN):
                    col = cols[i - p][k]
                    if i == p:
                        col = jnp.where(rowis > k, col, 0.0)
                        keep = jnp.where((lanes == lead + k) & (rowis > k), 0.0, rows[i])
                        keep = jnp.where((lanes == lead + k) & (rowis == k), 1.0, keep)
                    else:
                        keep = jnp.where(lanes == lead + k, 0.0, rows[i])
                    scaled = col * inv
                    rows[i] = keep - scaled * source
                    for m in range(k + 1, PAN):
                        cols[i - p][m] = cols[i - p][m] - scaled * raw[m - k - 1]
            rows[p] = rows[p] * lax.rsqrt(diag)
        whole = jnp.concatenate(rows, axis=0)
        lane = lax.broadcasted_iota(jnp.int32, (SUP, BLOCK), 1)
        row = lax.broadcasted_iota(jnp.int32, (SUP, BLOCK), 0) + first
        low = jnp.where((lane > row) & (lane < first + SUP), 0.0, whole)
        last = first + SUP
        if last < BLOCK:
            x_ref[first:last, :] = jnp.where(lane > row, 0.0, whole)
            flip = whole.T
            delta = jnp.concatenate([lax.dot_general(flip[r : r + SUP, :], low, (((1,), (0,)), ((), ())), precision=HI, preferred_element_type=jnp.float32) for r in range(last, BLOCK, SUP)], axis=0)
            lane_b = lax.broadcasted_iota(jnp.int32, (BLOCK - last, BLOCK), 1)
            below = x_ref[last:BLOCK, :]
            below = jnp.where((lane_b >= first) & (lane_b < last), 0.0, below)
            x_ref[last:BLOCK, :] = below - delta
        else:
            x_ref[first:last, :] = low
    return x_ref[...]

def start_of(n, j):
    return BLOCK * sum(n - i for i in range(j))

def basis_kernel(gram_ref, rows_ref, own_ref, away_ref, a_ref, s_ref, x_ref):
    n = rows_ref.shape[1] // BLOCK
    a_ref[...] = gram_ref[...]
    s_ref[...] = rows_ref[...]
    for k in range(n):
        base = start_of(n, k)
        x_ref[...] = a_ref[base : base + BLOCK, :]
        w = inverse_factor(x_ref)
        tail = s_ref[:, k * BLOCK : (k + 1) * BLOCK]
        below = (n - 1 - k) * BLOCK
        if below:
            stacked = jnp.concatenate([a_ref[base + BLOCK : base + BLOCK + below, :], tail], axis=0)
        else:
            stacked = tail
        panel = nt(stacked, w)
        solved = panel[below:, :] * float(M)
        share = solved.shape[0] // 2
        own_ref[:, k * BLOCK : (k + 1) * BLOCK] = solved[:share, :]
        away_ref[:, k * BLOCK : (k + 1) * BLOCK] = solved[share:, :]
        for j in range(k + 1, n):
            off = (j - k - 1) * BLOCK
            update = nt(panel[off:, :], panel[off : off + BLOCK, :])
            height = (n - j) * BLOCK
            to = start_of(n, j)
            a_ref[to : to + height, :] = a_ref[to : to + height, :] - update[:height, :]
            s_ref[:, j * BLOCK : (j + 1) * BLOCK] = s_ref[:, j * BLOCK : (j + 1) * BLOCK] - update[height:, :]

def basis(gram, rows):
    return pl.pallas_call(
        basis_kernel,
        out_shape=(in_vmem((rows.shape[0] // 2, rows.shape[1])),) * 2,
        in_specs=[vmem(), vmem()],
        out_specs=(vmem(), vmem()),
        compiler_params=pltpu.CompilerParams(vmem_limit_bytes=GRANT),
        scratch_shapes=[pltpu.VMEM(gram.shape, jnp.float32), pltpu.VMEM(rows.shape, jnp.float32), pltpu.VMEM((BLOCK, BLOCK), jnp.float32)],
        name="basis",
    )(gram, rows)


def vmem():
    return pl.BlockSpec(memory_space=pltpu.VMEM)


def in_vmem(shape):
    return pltpu.VMEM(shape, jnp.float32)


def held(x):
    return pltpu.with_memory_space_constraint(x, pltpu.VMEM)


def product_kernel(pattern_ref, weights_ref, sketch_ref, out_ref):
    layers, height, width = weights_ref.shape
    peers, _, share, rank = out_ref.shape
    for layer in range(layers):
        strips = []
        for i in range(height // BLOCK):
            parts = []
            for j in range(width // BLOCK):
                block = weights_ref[layer, i * BLOCK : (i + 1) * BLOCK, j * BLOCK : (j + 1) * BLOCK]
                parts.append(jnp.where(pattern_ref[j, layer, i] == 1, jnp.zeros_like(block), block))
            strips.append(jnp.concatenate(parts, axis=1))
        leftover = jnp.concatenate(strips, axis=0)
        product = jnp.dot(leftover, sketch_ref[...], preferred_element_type=jnp.float32)
        out_ref[:, layer] = product.reshape(peers, share, rank)


def product(weights, pattern, sketch, peers):
    layers, height, width = weights.shape
    rank = sketch.shape[1]
    return pl.pallas_call(
        product_kernel,
        out_shape=in_vmem((peers, layers, height // peers, rank)),
        in_specs=[pl.BlockSpec(memory_space=pltpu.SMEM), vmem(), vmem()],
        out_specs=vmem(),
        compiler_params=pltpu.CompilerParams(vmem_limit_bytes=GRANT),
        name="product",
    )(pattern, weights, sketch)


def total_kernel(core_ref, parts_ref, mine_ref, other_ref):
    core = core_ref[0]
    peers = parts_ref.shape[0]
    for layer, out_ref in ((core, mine_ref), (1 - core, other_ref)):
        total = parts_ref[0, layer]
        for peer in range(1, peers):
            total = total + parts_ref[peer, layer]
        out_ref[...] = total


def total(core, parts):
    shape = in_vmem(parts.shape[2:])
    return pl.pallas_call(
        total_kernel,
        out_shape=(shape, shape),
        in_specs=[pl.BlockSpec(memory_space=pltpu.SMEM), vmem()],
        out_specs=(vmem(), vmem()),
        compiler_params=pltpu.CompilerParams(vmem_limit_bytes=GRANT),
        name="total",
    )(core, held(parts))


def merge_kernel(core_ref, own_ref, back_ref, out_ref):
    core = core_ref[0]
    out_ref[core] = own_ref[...]
    out_ref[1 - core] = back_ref[...]


def merge(core, own, back):
    return pl.pallas_call(
        merge_kernel,
        out_shape=jax.ShapeDtypeStruct((LAYERS, *own.shape), jnp.float32),
        in_specs=[pl.BlockSpec(memory_space=pltpu.SMEM), vmem(), vmem()],
        out_specs=vmem(),
        compiler_params=pltpu.CompilerParams(vmem_limit_bytes=GRANT),
        name="merge",
    )(core, held(own), held(back))


def gram_kernel(mine_ref, got_ref, gram_ref, rows_ref):
    rows = jnp.concatenate([mine_ref[...], got_ref[...]], axis=0)
    rows_ref[...] = rows
    n = rows.shape[1] // BLOCK
    for j in range(n):
        to = start_of(n, j)
        gram_ref[to : to + (n - j) * BLOCK, :] = tn(rows[:, j * BLOCK :], rows[:, j * BLOCK : (j + 1) * BLOCK])


def local_gram(mine, got):
    share, rank = mine.shape
    n = rank // BLOCK
    return pl.pallas_call(
        gram_kernel,
        out_shape=(
            in_vmem((start_of(n, n), BLOCK)),
            in_vmem((2 * share, rank)),
        ),
        in_specs=[vmem(), vmem()],
        out_specs=(vmem(), vmem()),
        compiler_params=pltpu.CompilerParams(vmem_limit_bytes=GRANT),
        name="local_gram",
    )(held(mine), held(got))


def make_body(row_size, peers):
    chips = row_size // 2
    cores = [(2 * z + c, 2 * z + 1 - c) for z in range(chips) for c in range(2)]
    near = math.isqrt(chips)
    far = chips // near
    near_groups = [[2 * (h * near + l) + c for l in range(near)] for h in range(far) for c in range(2)]
    far_groups = [[2 * (h * near + l) + c for h in range(far)] for l in range(near) for c in range(2)]

    def to_col(x):
        return lax.all_to_all(x, "col", 0, 0)

    def to_near(x):
        return lax.all_to_all(x, "row", 0, 0, axis_index_groups=near_groups)

    def to_far(x):
        return lax.all_to_all(x, "row", 0, 0, axis_index_groups=far_groups)

    def spread(x, exchange, count):
        return exchange(jnp.broadcast_to(x, (count, *x.shape)))

    def summed_gram(gram):
        piece = jnp.sum(to_col(gram.reshape(peers, gram.shape[0] // peers, BLOCK)), axis=0)
        piece = jnp.sum(spread(piece, to_near, near), axis=0)
        piece = jnp.sum(spread(piece, to_far, far), axis=0)
        return spread(piece, to_col, peers).reshape(gram.shape)

    def body(weights, pattern, sketch):
        core = (lax.axis_index("row") % 2).astype(jnp.int32).reshape(1)
        pattern, core = lax.optimization_barrier((pattern.transpose(2, 0, 1), core))
        mine, other = total(core, to_col(product(weights, pattern, sketch, peers)))
        got = lax.ppermute(other, "row", cores)
        gram, rows = local_gram(mine, got)
        own, away = basis(held(summed_gram(gram)), held(rows))
        back = lax.ppermute(away, "row", cores)
        return merge(core, own, back)

    return body


def solution(mesh):
    return jax.shard_map(
        make_body(mesh.shape["row"], mesh.shape["col"]),
        mesh=mesh,
        in_specs=(P(None, "row", "col"), P(None, "row", "col"), P("col", None)),
        out_specs=P(None, ("row", "col"), None),
        check_vma=False,
    )
```

```python
import math

import jax
import jax.numpy as jnp
from jax import lax
from jax.experimental import pallas as pl
from jax.experimental.pallas import tpu as pltpu
from jax.sharding import PartitionSpec as P

M = 24576
BLOCK = 128
LAYERS = 2
SUP = 32
PAN = 16
GRANT = 24 << 20
PARTS = 2
HI = lax.Precision.HIGHEST


def nt(a, b):
    return lax.dot_general(a, b, (((1,), (1,)), ((), ())), precision=HI, preferred_element_type=jnp.float32)
def tn(a, b):
    return lax.dot_general(a, b, (((0,), (0,)), ((), ())), precision=HI, preferred_element_type=jnp.float32)

def inverse_factor(x_ref):
    lanes = lax.broadcasted_iota(jnp.int32, (PAN, BLOCK), 1)
    rowis = lax.broadcasted_iota(jnp.int32, (PAN, BLOCK), 0)
    for first in range(0, BLOCK, SUP):
        rows = [x_ref[first + PAN * i : first + PAN * (i + 1), :] for i in range(SUP // PAN)]
        for p in range(SUP // PAN):
            lead = first + PAN * p
            cols = [[jnp.broadcast_to(rows[i][:, lead + k : lead + k + 1], (PAN, BLOCK)) for k in range(PAN)] for i in range(p, SUP // PAN)]
            diag = jnp.ones((PAN, BLOCK), jnp.float32)
            for k in range(PAN):
                pivot = jnp.broadcast_to(cols[0][k][k : k + 1, :], (PAN, BLOCK))
                inv = 1.0 / pivot
                diag = jnp.where(rowis == k, pivot, diag)
                source = jnp.where(lanes == lead + k, 1.0, jnp.broadcast_to(rows[p][k : k + 1, :], (PAN, BLOCK)))
                raw = [jnp.broadcast_to(cols[0][k][m : m + 1, :], (PAN, BLOCK)) for m in range(k + 1, PAN)]
                for i in range(p, SUP // PAN):
                    col = cols[i - p][k]
                    if i == p:
                        col = jnp.where(rowis > k, col, 0.0)
                        keep = jnp.where((lanes == lead + k) & (rowis > k), 0.0, rows[i])
                        keep = jnp.where((lanes == lead + k) & (rowis == k), 1.0, keep)
                    else:
                        keep = jnp.where(lanes == lead + k, 0.0, rows[i])
                    scaled = col * inv
                    rows[i] = keep - scaled * source
                    for m in range(k + 1, PAN):
                        cols[i - p][m] = cols[i - p][m] - scaled * raw[m - k - 1]
            rows[p] = rows[p] * lax.rsqrt(diag)
        whole = jnp.concatenate(rows, axis=0)
        lane = lax.broadcasted_iota(jnp.int32, (SUP, BLOCK), 1)
        row = lax.broadcasted_iota(jnp.int32, (SUP, BLOCK), 0) + first
        low = jnp.where((lane > row) & (lane < first + SUP), 0.0, whole)
        last = first + SUP
        if last < BLOCK:
            x_ref[first:last, :] = jnp.where(lane > row, 0.0, whole)
            flip = whole.T
            delta = jnp.concatenate([lax.dot_general(flip[r : r + SUP, :], low, (((1,), (0,)), ((), ())), precision=HI, preferred_element_type=jnp.float32) for r in range(last, BLOCK, SUP)], axis=0)
            lane_b = lax.broadcasted_iota(jnp.int32, (BLOCK - last, BLOCK), 1)
            below = x_ref[last:BLOCK, :]
            below = jnp.where((lane_b >= first) & (lane_b < last), 0.0, below)
            x_ref[last:BLOCK, :] = below - delta
        else:
            x_ref[first:last, :] = low
    return x_ref[...]

def start_of(n, j):
    return BLOCK * sum(n - i for i in range(j))

def basis_kernel(gram_ref, rows_ref, own_ref, away_ref, a_ref, s_ref, x_ref):
    n = rows_ref.shape[1] // BLOCK
    a_ref[...] = gram_ref[...]
    s_ref[...] = rows_ref[...]
    for k in range(n):
        base = start_of(n, k)
        x_ref[...] = a_ref[base : base + BLOCK, :]
        w = inverse_factor(x_ref)
        tail = s_ref[:, k * BLOCK : (k + 1) * BLOCK]
        below = (n - 1 - k) * BLOCK
        if below:
            stacked = jnp.concatenate([a_ref[base + BLOCK : base + BLOCK + below, :], tail], axis=0)
        else:
            stacked = tail
        panel = nt(stacked, w)
        solved = panel[below:, :] * float(M)
        share = solved.shape[0] // 2
        own_ref[:, k * BLOCK : (k + 1) * BLOCK] = solved[:share, :]
        away_ref[:, k * BLOCK : (k + 1) * BLOCK] = solved[share:, :]
        for j in range(k + 1, n):
            off = (j - k - 1) * BLOCK
            update = nt(panel[off:, :], panel[off : off + BLOCK, :])
            height = (n - j) * BLOCK
            to = start_of(n, j)
            a_ref[to : to + height, :] = a_ref[to : to + height, :] - update[:height, :]
            s_ref[:, j * BLOCK : (j + 1) * BLOCK] = s_ref[:, j * BLOCK : (j + 1) * BLOCK] - update[height:, :]

def basis(gram, rows):
    return pl.pallas_call(
        basis_kernel,
        out_shape=(in_vmem((rows.shape[0] // 2, rows.shape[1])),) * 2,
        in_specs=[vmem(), vmem()],
        out_specs=(vmem(), vmem()),
        compiler_params=pltpu.CompilerParams(vmem_limit_bytes=GRANT),
        scratch_shapes=[pltpu.VMEM(gram.shape, jnp.float32), pltpu.VMEM(rows.shape, jnp.float32), pltpu.VMEM((BLOCK, BLOCK), jnp.float32)],
        name="basis",
    )(gram, rows)


def vmem():
    return pl.BlockSpec(memory_space=pltpu.VMEM)


def in_vmem(shape):
    return pltpu.VMEM(shape, jnp.float32)


def held(x):
    return pltpu.with_memory_space_constraint(x, pltpu.VMEM)


def product_kernel(pattern_hbm, weights_hbm, sketch_hbm, out_ref, pattern_ref, weights_ref, sketch_ref, sems):
    layers, height, width = weights_ref.shape
    peers, _, share, rank = out_ref.shape
    part = height // PARTS
    copies = [
        pltpu.make_async_copy(pattern_hbm, pattern_ref, sems.at[0]),
        pltpu.make_async_copy(sketch_hbm, sketch_ref, sems.at[1]),
    ]
    for layer in range(layers):
        for h in range(PARTS):
            rows = pl.ds(h * part, part)
            copies.append(pltpu.make_async_copy(weights_hbm.at[layer, rows], weights_ref.at[layer, rows], sems.at[len(copies)]))
    for copy in copies:
        copy.start()
    copies[0].wait()
    copies[1].wait()
    for layer in range(layers):
        for h in range(PARTS):
            copies[2 + layer * PARTS + h].wait()
            strips = []
            for i in range(h * part // BLOCK, (h + 1) * part // BLOCK):
                parts = []
                for j in range(width // BLOCK):
                    block = weights_ref[layer, i * BLOCK : (i + 1) * BLOCK, j * BLOCK : (j + 1) * BLOCK]
                    parts.append(jnp.where(pattern_ref[j, layer, i] == 1, jnp.zeros_like(block), block))
                strips.append(jnp.concatenate(parts, axis=1))
            leftover = jnp.concatenate(strips, axis=0)
            product = jnp.dot(leftover, sketch_ref[...], preferred_element_type=jnp.float32)
            out_ref[h * peers // PARTS : (h + 1) * peers // PARTS, layer] = product.reshape(peers // PARTS, share, rank)


def product(weights, pattern, sketch, peers):
    layers, height, width = weights.shape
    rank = sketch.shape[1]
    anywhere = pl.BlockSpec(memory_space=pltpu.HBM)
    return pl.pallas_call(
        product_kernel,
        out_shape=in_vmem((peers, layers, height // peers, rank)),
        in_specs=[anywhere] * 3,
        out_specs=vmem(),
        scratch_shapes=[
            pltpu.SMEM(pattern.shape, jnp.int32),
            pltpu.VMEM(weights.shape, weights.dtype),
            pltpu.VMEM(sketch.shape, sketch.dtype),
            pltpu.SemaphoreType.DMA((2 + layers * PARTS,)),
        ],
        compiler_params=pltpu.CompilerParams(vmem_limit_bytes=GRANT),
        name="product",
    )(*(pltpu.with_memory_space_constraint(x, pltpu.HBM) for x in (pattern, weights, sketch)))


def total_kernel(core_ref, parts_ref, mine_ref, other_ref):
    core = core_ref[0]
    peers = parts_ref.shape[0]
    for layer, out_ref in ((core, mine_ref), (1 - core, other_ref)):
        total = parts_ref[0, layer]
        for peer in range(1, peers):
            total = total + parts_ref[peer, layer]
        out_ref[...] = total


def total(core, parts):
    shape = in_vmem(parts.shape[2:])
    return pl.pallas_call(
        total_kernel,
        out_shape=(shape, shape),
        in_specs=[pl.BlockSpec(memory_space=pltpu.SMEM), vmem()],
        out_specs=(vmem(), vmem()),
        compiler_params=pltpu.CompilerParams(vmem_limit_bytes=GRANT),
        name="total",
    )(core, held(parts))


def merge_kernel(core_ref, own_ref, back_ref, out_ref):
    core = core_ref[0]
    out_ref[core] = own_ref[...]
    out_ref[1 - core] = back_ref[...]


def merge(core, own, back):
    return pl.pallas_call(
        merge_kernel,
        out_shape=jax.ShapeDtypeStruct((LAYERS, *own.shape), jnp.float32),
        in_specs=[pl.BlockSpec(memory_space=pltpu.SMEM), vmem(), vmem()],
        out_specs=vmem(),
        compiler_params=pltpu.CompilerParams(vmem_limit_bytes=GRANT),
        name="merge",
    )(core, held(own), held(back))


def gram_kernel(mine_ref, got_ref, gram_ref, rows_ref):
    rows = jnp.concatenate([mine_ref[...], got_ref[...]], axis=0)
    rows_ref[...] = rows
    n = rows.shape[1] // BLOCK
    for j in range(n):
        to = start_of(n, j)
        gram_ref[to : to + (n - j) * BLOCK, :] = tn(rows[:, j * BLOCK :], rows[:, j * BLOCK : (j + 1) * BLOCK])


def local_gram(mine, got):
    share, rank = mine.shape
    n = rank // BLOCK
    return pl.pallas_call(
        gram_kernel,
        out_shape=(
            in_vmem((start_of(n, n), BLOCK)),
            in_vmem((2 * share, rank)),
        ),
        in_specs=[vmem(), vmem()],
        out_specs=(vmem(), vmem()),
        compiler_params=pltpu.CompilerParams(vmem_limit_bytes=GRANT),
        name="local_gram",
    )(held(mine), held(got))


def make_body(row_size, peers):
    chips = row_size // 2
    cores = [(2 * z + c, 2 * z + 1 - c) for z in range(chips) for c in range(2)]
    near = math.isqrt(chips)
    far = chips // near
    near_groups = [[2 * (h * near + l) + c for l in range(near)] for h in range(far) for c in range(2)]
    far_groups = [[2 * (h * near + l) + c for h in range(far)] for l in range(near) for c in range(2)]

    def to_col(x):
        return lax.all_to_all(x, "col", 0, 0)

    def to_near(x):
        return lax.all_to_all(x, "row", 0, 0, axis_index_groups=near_groups)

    def to_far(x):
        return lax.all_to_all(x, "row", 0, 0, axis_index_groups=far_groups)

    def spread(x, exchange, count):
        return exchange(jnp.broadcast_to(x, (count, *x.shape)))

    def summed_gram(gram):
        piece = jnp.sum(to_col(gram.reshape(peers, gram.shape[0] // peers, BLOCK)), axis=0)
        piece = jnp.sum(spread(piece, to_near, near), axis=0)
        piece = jnp.sum(spread(piece, to_far, far), axis=0)
        return spread(piece, to_col, peers).reshape(gram.shape)

    def body(weights, pattern, sketch):
        core = (lax.axis_index("row") % 2).astype(jnp.int32).reshape(1)
        pattern, core = lax.optimization_barrier((pattern.transpose(2, 0, 1), core))
        mine, other = total(core, to_col(product(weights, pattern, sketch, peers)))
        got = lax.ppermute(other, "row", cores)
        gram, rows = local_gram(mine, got)
        own, away = basis(held(summed_gram(gram)), held(rows))
        back = lax.ppermute(away, "row", cores)
        return merge(core, own, back)

    return body


def solution(mesh):
    return jax.shard_map(
        make_body(mesh.shape["row"], mesh.shape["col"]),
        mesh=mesh,
        in_specs=(P(None, "row", "col"), P(None, "row", "col"), P("col", None)),
        out_specs=P(None, ("row", "col"), None),
        check_vma=False,
    )
```

```python
import math

import jax
import jax.numpy as jnp
from jax import lax
from jax.experimental import pallas as pl
from jax.experimental.pallas import tpu as pltpu
from jax.sharding import PartitionSpec as P

M = 24576
BLOCK = 128
LAYERS = 2
SUP = 32
PAN = 16
GRANT = 24 << 20
PARTS = 2
HI = lax.Precision.HIGHEST


def nt(a, b):
    return lax.dot_general(a, b, (((1,), (1,)), ((), ())), precision=HI, preferred_element_type=jnp.float32)
def tn(a, b):
    return lax.dot_general(a, b, (((0,), (0,)), ((), ())), precision=HI, preferred_element_type=jnp.float32)

def inverse_factor(x_ref):
    lanes = lax.broadcasted_iota(jnp.int32, (PAN, BLOCK), 1)
    rowis = lax.broadcasted_iota(jnp.int32, (PAN, BLOCK), 0)
    for first in range(0, BLOCK, SUP):
        rows = [x_ref[first + PAN * i : first + PAN * (i + 1), :] for i in range(SUP // PAN)]
        for p in range(SUP // PAN):
            lead = first + PAN * p
            cols = [[jnp.broadcast_to(rows[i][:, lead + k : lead + k + 1], (PAN, BLOCK)) for k in range(PAN)] for i in range(p, SUP // PAN)]
            diag = jnp.ones((PAN, BLOCK), jnp.float32)
            for k in range(PAN):
                pivot = jnp.broadcast_to(cols[0][k][k : k + 1, :], (PAN, BLOCK))
                inv = 1.0 / pivot
                diag = jnp.where(rowis == k, pivot, diag)
                source = jnp.where(lanes == lead + k, 1.0, jnp.broadcast_to(rows[p][k : k + 1, :], (PAN, BLOCK)))
                raw = [jnp.broadcast_to(cols[0][k][m : m + 1, :], (PAN, BLOCK)) for m in range(k + 1, PAN)]
                for i in range(p, SUP // PAN):
                    col = cols[i - p][k]
                    if i == p:
                        col = jnp.where(rowis > k, col, 0.0)
                        keep = jnp.where((lanes == lead + k) & (rowis > k), 0.0, rows[i])
                        keep = jnp.where((lanes == lead + k) & (rowis == k), 1.0, keep)
                    else:
                        keep = jnp.where(lanes == lead + k, 0.0, rows[i])
                    scaled = col * inv
                    rows[i] = keep - scaled * source
                    for m in range(k + 1, PAN):
                        cols[i - p][m] = cols[i - p][m] - scaled * raw[m - k - 1]
            rows[p] = rows[p] * lax.rsqrt(diag)
        whole = jnp.concatenate(rows, axis=0)
        lane = lax.broadcasted_iota(jnp.int32, (SUP, BLOCK), 1)
        row = lax.broadcasted_iota(jnp.int32, (SUP, BLOCK), 0) + first
        low = jnp.where((lane > row) & (lane < first + SUP), 0.0, whole)
        last = first + SUP
        if last < BLOCK:
            x_ref[first:last, :] = jnp.where(lane > row, 0.0, whole)
            flip = whole.T
            delta = jnp.concatenate([lax.dot_general(flip[r : r + SUP, :], low, (((1,), (0,)), ((), ())), precision=HI, preferred_element_type=jnp.float32) for r in range(last, BLOCK, SUP)], axis=0)
            lane_b = lax.broadcasted_iota(jnp.int32, (BLOCK - last, BLOCK), 1)
            below = x_ref[last:BLOCK, :]
            below = jnp.where((lane_b >= first) & (lane_b < last), 0.0, below)
            x_ref[last:BLOCK, :] = below - delta
        else:
            x_ref[first:last, :] = low
    return x_ref[...]

def start_of(n, j):
    return BLOCK * sum(n - i for i in range(j))

def basis_kernel(gram_ref, rows_ref, out_ref, a_ref, s_ref, x_ref):
    count, share, rank = rows_ref.shape
    n = rank // BLOCK
    a_ref[...] = gram_ref[...]
    s_ref[...] = rows_ref[...].reshape(count * share, rank)
    for k in range(n):
        base = start_of(n, k)
        x_ref[...] = a_ref[base : base + BLOCK, :]
        w = inverse_factor(x_ref)
        tail = s_ref[:, k * BLOCK : (k + 1) * BLOCK]
        below = (n - 1 - k) * BLOCK
        if below:
            stacked = jnp.concatenate([a_ref[base + BLOCK : base + BLOCK + below, :], tail], axis=0)
        else:
            stacked = tail
        panel = nt(stacked, w)
        solved = panel[below:, :] * float(M)
        out_ref[:, :, k * BLOCK : (k + 1) * BLOCK] = solved.reshape(count, share, BLOCK)
        for j in range(k + 1, n):
            off = (j - k - 1) * BLOCK
            update = nt(panel[off:, :], panel[off : off + BLOCK, :])
            height = (n - j) * BLOCK
            to = start_of(n, j)
            a_ref[to : to + height, :] = a_ref[to : to + height, :] - update[:height, :]
            s_ref[:, j * BLOCK : (j + 1) * BLOCK] = s_ref[:, j * BLOCK : (j + 1) * BLOCK] - update[height:, :]

def basis(gram, rows):
    count, share, rank = rows.shape
    return pl.pallas_call(
        basis_kernel,
        out_shape=in_vmem(rows.shape),
        in_specs=[vmem(), vmem()],
        out_specs=vmem(),
        scratch_shapes=[pltpu.VMEM(gram.shape, jnp.float32), pltpu.VMEM((count * share, rank), jnp.float32), pltpu.VMEM((BLOCK, BLOCK), jnp.float32)],
        compiler_params=pltpu.CompilerParams(vmem_limit_bytes=GRANT),
        name="basis",
    )(gram, rows)


def vmem():
    return pl.BlockSpec(memory_space=pltpu.VMEM)


def in_vmem(shape):
    return pltpu.VMEM(shape, jnp.float32)


def held(x):
    return pltpu.with_memory_space_constraint(x, pltpu.VMEM)


def product_kernel(pattern_hbm, weights_hbm, sketch_hbm, out_ref, pattern_ref, weights_ref, sketch_ref, sems):
    layers, height, width = weights_ref.shape
    peers, _, share, rank = out_ref.shape
    part = height // PARTS
    copies = [
        pltpu.make_async_copy(pattern_hbm, pattern_ref, sems.at[0]),
        pltpu.make_async_copy(sketch_hbm, sketch_ref, sems.at[1]),
    ]
    for layer in range(layers):
        for h in range(PARTS):
            rows = pl.ds(h * part, part)
            copies.append(pltpu.make_async_copy(weights_hbm.at[layer, rows], weights_ref.at[layer, rows], sems.at[len(copies)]))
    for copy in copies:
        copy.start()
    copies[0].wait()
    copies[1].wait()
    for layer in range(layers):
        for h in range(PARTS):
            copies[2 + layer * PARTS + h].wait()
            strips = []
            for i in range(h * part // BLOCK, (h + 1) * part // BLOCK):
                parts = []
                for j in range(width // BLOCK):
                    block = weights_ref[layer, i * BLOCK : (i + 1) * BLOCK, j * BLOCK : (j + 1) * BLOCK]
                    parts.append(jnp.where(pattern_ref[j, layer, i] == 1, jnp.zeros_like(block), block))
                strips.append(jnp.concatenate(parts, axis=1))
            leftover = jnp.concatenate(strips, axis=0)
            product = jnp.dot(leftover, sketch_ref[...], preferred_element_type=jnp.float32)
            out_ref[h * peers // PARTS : (h + 1) * peers // PARTS, layer] = product.reshape(peers // PARTS, share, rank)


def product(weights, pattern, sketch, peers):
    layers, height, width = weights.shape
    rank = sketch.shape[1]
    anywhere = pl.BlockSpec(memory_space=pltpu.HBM)
    return pl.pallas_call(
        product_kernel,
        out_shape=in_vmem((peers, layers, height // peers, rank)),
        in_specs=[anywhere] * 3,
        out_specs=vmem(),
        scratch_shapes=[
            pltpu.SMEM(pattern.shape, jnp.int32),
            pltpu.VMEM(weights.shape, weights.dtype),
            pltpu.VMEM(sketch.shape, sketch.dtype),
            pltpu.SemaphoreType.DMA((2 + layers * PARTS,)),
        ],
        compiler_params=pltpu.CompilerParams(vmem_limit_bytes=GRANT),
        name="product",
    )(*(pltpu.with_memory_space_constraint(x, pltpu.HBM) for x in (pattern, weights, sketch)))


def total_kernel(parts_ref, out_ref):
    total = parts_ref[0]
    for peer in range(1, parts_ref.shape[0]):
        total = total + parts_ref[peer]
    out_ref[...] = total


def total(parts):
    return pl.pallas_call(
        total_kernel,
        out_shape=in_vmem(parts.shape[1:]),
        in_specs=[vmem()],
        out_specs=vmem(),
        compiler_params=pltpu.CompilerParams(vmem_limit_bytes=GRANT),
        name="total",
    )(held(parts))


def gram_kernel(rows_ref, gram_ref):
    rows = rows_ref[...].reshape(-1, rows_ref.shape[-1])
    n = rows.shape[1] // BLOCK
    for j in range(n):
        to = start_of(n, j)
        gram_ref[to : to + (n - j) * BLOCK, :] = tn(rows[:, j * BLOCK :], rows[:, j * BLOCK : (j + 1) * BLOCK])


def local_gram(rows):
    n = rows.shape[-1] // BLOCK
    return pl.pallas_call(
        gram_kernel,
        out_shape=in_vmem((start_of(n, n), BLOCK)),
        in_specs=[vmem()],
        out_specs=vmem(),
        compiler_params=pltpu.CompilerParams(vmem_limit_bytes=GRANT),
        name="local_gram",
    )(rows)


def make_body(row_size, peers):
    chips = row_size // 2
    pairs = [[2 * z, 2 * z + 1] for z in range(chips)]
    near = math.isqrt(chips)
    far = chips // near
    near_groups = [[2 * (h * near + l) + c for l in range(near)] for h in range(far) for c in range(2)]
    far_groups = [[2 * (h * near + l) + c for h in range(far)] for l in range(near) for c in range(2)]

    def to_col(x):
        return lax.all_to_all(x, "col", 0, 0)

    def swap(x):
        return lax.all_to_all(x, "row", 0, 0, axis_index_groups=pairs)

    def to_near(x):
        return lax.all_to_all(x, "row", 0, 0, axis_index_groups=near_groups)

    def to_far(x):
        return lax.all_to_all(x, "row", 0, 0, axis_index_groups=far_groups)

    def spread(x, exchange, count):
        return exchange(jnp.broadcast_to(x, (count, *x.shape)))

    def summed_gram(gram):
        piece = jnp.sum(to_col(gram.reshape(peers, gram.shape[0] // peers, BLOCK)), axis=0)
        piece = jnp.sum(spread(piece, to_near, near), axis=0)
        piece = jnp.sum(spread(piece, to_far, far), axis=0)
        return spread(piece, to_col, peers).reshape(gram.shape)

    def body(weights, pattern, sketch):
        sampled = total(to_col(product(weights, pattern.transpose(2, 0, 1), sketch, peers)))
        rows = held(swap(sampled))
        return swap(basis(held(summed_gram(local_gram(rows))), rows))

    return body


def solution(mesh):
    return jax.shard_map(
        make_body(mesh.shape["row"], mesh.shape["col"]),
        mesh=mesh,
        in_specs=(P(None, "row", "col"), P(None, "row", "col"), P("col", None)),
        out_specs=P(None, ("row", "col"), None),
        check_vma=False,
    )
```

```python
import math

import jax
import jax.numpy as jnp
from jax import lax
from jax.experimental import pallas as pl
from jax.experimental.pallas import tpu as pltpu
from jax.sharding import PartitionSpec as P

M = 24576
BLOCK = 128
LAYERS = 2
SUP = 32
PAN = 16
GRANT = 24 << 20
PARTS = 2
HI = lax.Precision.HIGHEST


def nt(a, b):
    return lax.dot_general(a, b, (((1,), (1,)), ((), ())), precision=HI, preferred_element_type=jnp.float32)
def tn(a, b):
    return lax.dot_general(a, b, (((0,), (0,)), ((), ())), precision=HI, preferred_element_type=jnp.float32)

def inverse_factor(x_ref):
    lanes = lax.broadcasted_iota(jnp.int32, (PAN, BLOCK), 1)
    rowis = lax.broadcasted_iota(jnp.int32, (PAN, BLOCK), 0)
    for first in range(0, BLOCK, SUP):
        rows = [x_ref[first + PAN * i : first + PAN * (i + 1), :] for i in range(SUP // PAN)]
        for p in range(SUP // PAN):
            lead = first + PAN * p
            cols = [[jnp.broadcast_to(rows[i][:, lead + k : lead + k + 1], (PAN, BLOCK)) for k in range(PAN)] for i in range(p, SUP // PAN)]
            diag = jnp.ones((PAN, BLOCK), jnp.float32)
            for k in range(PAN):
                pivot = jnp.broadcast_to(cols[0][k][k : k + 1, :], (PAN, BLOCK))
                inv = 1.0 / pivot
                diag = jnp.where(rowis == k, pivot, diag)
                source = jnp.where(lanes == lead + k, 1.0, jnp.broadcast_to(rows[p][k : k + 1, :], (PAN, BLOCK)))
                raw = [jnp.broadcast_to(cols[0][k][m : m + 1, :], (PAN, BLOCK)) for m in range(k + 1, PAN)]
                for i in range(p, SUP // PAN):
                    col = cols[i - p][k]
                    if i == p:
                        col = jnp.where(rowis > k, col, 0.0)
                        keep = jnp.where((lanes == lead + k) & (rowis > k), 0.0, rows[i])
                        keep = jnp.where((lanes == lead + k) & (rowis == k), 1.0, keep)
                    else:
                        keep = jnp.where(lanes == lead + k, 0.0, rows[i])
                    scaled = col * inv
                    rows[i] = keep - scaled * source
                    for m in range(k + 1, PAN):
                        cols[i - p][m] = cols[i - p][m] - scaled * raw[m - k - 1]
            rows[p] = rows[p] * lax.rsqrt(diag)
        whole = jnp.concatenate(rows, axis=0)
        lane = lax.broadcasted_iota(jnp.int32, (SUP, BLOCK), 1)
        row = lax.broadcasted_iota(jnp.int32, (SUP, BLOCK), 0) + first
        low = jnp.where((lane > row) & (lane < first + SUP), 0.0, whole)
        last = first + SUP
        if last < BLOCK:
            x_ref[first:last, :] = jnp.where(lane > row, 0.0, whole)
            flip = whole.T
            delta = jnp.concatenate([lax.dot_general(flip[r : r + SUP, :], low, (((1,), (0,)), ((), ())), precision=HI, preferred_element_type=jnp.float32) for r in range(last, BLOCK, SUP)], axis=0)
            lane_b = lax.broadcasted_iota(jnp.int32, (BLOCK - last, BLOCK), 1)
            below = x_ref[last:BLOCK, :]
            below = jnp.where((lane_b >= first) & (lane_b < last), 0.0, below)
            x_ref[last:BLOCK, :] = below - delta
        else:
            x_ref[first:last, :] = low
    return x_ref[...]

def start_of(n, j):
    return BLOCK * sum(n - i for i in range(j))

def basis_kernel(gram_ref, rows_ref, own_ref, away_ref, a_ref, s_ref, x_ref):
    n = rows_ref.shape[1] // BLOCK
    a_ref[...] = gram_ref[...]
    s_ref[...] = rows_ref[...]
    for k in range(n):
        base = start_of(n, k)
        x_ref[...] = a_ref[base : base + BLOCK, :]
        w = inverse_factor(x_ref)
        tail = s_ref[:, k * BLOCK : (k + 1) * BLOCK]
        below = (n - 1 - k) * BLOCK
        if below:
            stacked = jnp.concatenate([a_ref[base + BLOCK : base + BLOCK + below, :], tail], axis=0)
        else:
            stacked = tail
        panel = nt(stacked, w)
        solved = panel[below:, :] * float(M)
        share = solved.shape[0] // 2
        own_ref[:, k * BLOCK : (k + 1) * BLOCK] = solved[:share, :]
        away_ref[:, k * BLOCK : (k + 1) * BLOCK] = solved[share:, :]
        for j in range(k + 1, n):
            off = (j - k - 1) * BLOCK
            update = nt(panel[off:, :], panel[off : off + BLOCK, :])
            height = (n - j) * BLOCK
            to = start_of(n, j)
            a_ref[to : to + height, :] = a_ref[to : to + height, :] - update[:height, :]
            s_ref[:, j * BLOCK : (j + 1) * BLOCK] = s_ref[:, j * BLOCK : (j + 1) * BLOCK] - update[height:, :]

def basis(gram, rows):
    return pl.pallas_call(
        basis_kernel,
        out_shape=(in_vmem((rows.shape[0] // 2, rows.shape[1])),) * 2,
        in_specs=[vmem(), vmem()],
        out_specs=(vmem(), vmem()),
        compiler_params=pltpu.CompilerParams(vmem_limit_bytes=GRANT),
        scratch_shapes=[pltpu.VMEM(gram.shape, jnp.float32), pltpu.VMEM(rows.shape, jnp.float32), pltpu.VMEM((BLOCK, BLOCK), jnp.float32)],
        name="basis",
    )(gram, rows)


def vmem():
    return pl.BlockSpec(memory_space=pltpu.VMEM)


def in_vmem(shape):
    return pltpu.VMEM(shape, jnp.float32)


def held(x):
    return pltpu.with_memory_space_constraint(x, pltpu.VMEM)


def product_kernel(pattern_hbm, weights_hbm, sketch_hbm, out_ref, pattern_ref, weights_ref, sketch_ref, sems):
    layers, height, width = weights_ref.shape
    peers, _, share, rank = out_ref.shape
    part = height // PARTS
    copies = [
        pltpu.make_async_copy(pattern_hbm, pattern_ref, sems.at[0]),
        pltpu.make_async_copy(sketch_hbm, sketch_ref, sems.at[1]),
    ]
    for layer in range(layers):
        for h in range(PARTS):
            rows = pl.ds(h * part, part)
            copies.append(pltpu.make_async_copy(weights_hbm.at[layer, rows], weights_ref.at[layer, rows], sems.at[len(copies)]))
    for copy in copies:
        copy.start()
    copies[0].wait()
    copies[1].wait()
    for layer in range(layers):
        for h in range(PARTS):
            copies[2 + layer * PARTS + h].wait()
            strips = []
            for i in range(h * part // BLOCK, (h + 1) * part // BLOCK):
                parts = []
                for j in range(width // BLOCK):
                    block = weights_ref[layer, i * BLOCK : (i + 1) * BLOCK, j * BLOCK : (j + 1) * BLOCK]
                    parts.append(jnp.where(pattern_ref[j, layer, i] == 1, jnp.zeros_like(block), block))
                strips.append(jnp.concatenate(parts, axis=1))
            leftover = jnp.concatenate(strips, axis=0)
            product = jnp.dot(leftover, sketch_ref[...], preferred_element_type=jnp.float32)
            out_ref[h * peers // PARTS : (h + 1) * peers // PARTS, layer] = product.reshape(peers // PARTS, share, rank)


def product(weights, pattern, sketch, peers):
    layers, height, width = weights.shape
    rank = sketch.shape[1]
    anywhere = pl.BlockSpec(memory_space=pltpu.HBM)
    return pl.pallas_call(
        product_kernel,
        out_shape=in_vmem((peers, layers, height // peers, rank)),
        in_specs=[anywhere] * 3,
        out_specs=vmem(),
        scratch_shapes=[
            pltpu.SMEM(pattern.shape, jnp.int32),
            pltpu.VMEM(weights.shape, weights.dtype),
            pltpu.VMEM(sketch.shape, sketch.dtype),
            pltpu.SemaphoreType.DMA((2 + layers * PARTS,)),
        ],
        compiler_params=pltpu.CompilerParams(vmem_limit_bytes=GRANT),
        name="product",
    )(*(pltpu.with_memory_space_constraint(x, pltpu.HBM) for x in (pattern, weights, sketch)))


def total_kernel(core_ref, parts_ref, mine_ref, other_ref):
    core = core_ref[0]
    peers = parts_ref.shape[0]
    for layer, out_ref in ((core, mine_ref), (1 - core, other_ref)):
        total = parts_ref[0, layer]
        for peer in range(1, peers):
            total = total + parts_ref[peer, layer]
        out_ref[...] = total


def total(core, parts):
    shape = in_vmem(parts.shape[2:])
    return pl.pallas_call(
        total_kernel,
        out_shape=(shape, shape),
        in_specs=[pl.BlockSpec(memory_space=pltpu.SMEM), vmem()],
        out_specs=(vmem(), vmem()),
        compiler_params=pltpu.CompilerParams(vmem_limit_bytes=GRANT),
        name="total",
    )(core, held(parts))


def merge_kernel(core_ref, own_ref, back_ref, out_ref):
    core = core_ref[0]
    out_ref[core] = own_ref[...]
    out_ref[1 - core] = back_ref[...]


def merge(core, own, back):
    return pl.pallas_call(
        merge_kernel,
        out_shape=jax.ShapeDtypeStruct((LAYERS, *own.shape), jnp.float32),
        in_specs=[pl.BlockSpec(memory_space=pltpu.SMEM), vmem(), vmem()],
        out_specs=vmem(),
        compiler_params=pltpu.CompilerParams(vmem_limit_bytes=GRANT),
        name="merge",
    )(core, held(own), held(back))


def gram_kernel(mine_ref, got_ref, gram_ref, rows_ref):
    rows = jnp.concatenate([mine_ref[...], got_ref[...]], axis=0)
    rows_ref[...] = rows
    n = rows.shape[1] // BLOCK
    for j in range(n):
        to = start_of(n, j)
        gram_ref[to : to + (n - j) * BLOCK, :] = tn(rows[:, j * BLOCK :], rows[:, j * BLOCK : (j + 1) * BLOCK])


def local_gram(mine, got):
    share, rank = mine.shape
    n = rank // BLOCK
    return pl.pallas_call(
        gram_kernel,
        out_shape=(
            in_vmem((start_of(n, n), BLOCK)),
            in_vmem((2 * share, rank)),
        ),
        in_specs=[vmem(), vmem()],
        out_specs=(vmem(), vmem()),
        compiler_params=pltpu.CompilerParams(vmem_limit_bytes=GRANT),
        name="local_gram",
    )(held(mine), held(got))


def make_body(row_size, peers):
    chips = row_size // 2
    cores = [(2 * z + c, 2 * z + 1 - c) for z in range(chips) for c in range(2)]
    near = math.isqrt(chips)
    far = chips // near
    near_groups = [[2 * (h * near + l) + c for l in range(near)] for h in range(far) for c in range(2)]
    far_groups = [[2 * (h * near + l) + c for h in range(far)] for l in range(near) for c in range(2)]

    def to_col(x):
        return lax.all_to_all(x, "col", 0, 0)

    def to_near(x):
        return lax.all_to_all(x, "row", 0, 0, axis_index_groups=near_groups)

    def to_far(x):
        return lax.all_to_all(x, "row", 0, 0, axis_index_groups=far_groups)

    def spread(x, exchange, count):
        return exchange(jnp.broadcast_to(x, (count, *x.shape)))

    def summed_gram(gram):
        piece = jnp.sum(to_col(gram.reshape(peers, gram.shape[0] // peers, BLOCK)), axis=0)
        piece = jnp.sum(spread(piece, to_far, far), axis=0)
        piece = jnp.sum(spread(piece, to_near, near), axis=0)
        return spread(piece, to_col, peers).reshape(gram.shape)

    def body(weights, pattern, sketch):
        core = (lax.axis_index("row") % 2).astype(jnp.int32).reshape(1)
        pattern, core = lax.optimization_barrier((pattern.transpose(2, 0, 1), core))
        mine, other = total(core, to_col(product(weights, pattern, sketch, peers)))
        got = lax.ppermute(other, "row", cores)
        gram, rows = local_gram(mine, got)
        own, away = basis(held(summed_gram(gram)), held(rows))
        back = lax.ppermute(away, "row", cores)
        return merge(core, own, back)

    return body


def solution(mesh):
    return jax.shard_map(
        make_body(mesh.shape["row"], mesh.shape["col"]),
        mesh=mesh,
        in_specs=(P(None, "row", "col"), P(None, "row", "col"), P("col", None)),
        out_specs=P(None, ("row", "col"), None),
        check_vma=False,
    )
```
